32 devices in a mesh: cell: 16 (over z, x, core), gene: 2 (over y).
Axes of the slice: x: 2, y: 2, z: 4, core: 2. Of those that a mesh axis runs over, the one named last changes fastest.
Arguments:
- counts: bfloat16 [15360, 16384], P('cell', 'gene'), as said below
- w_factor: float32 [15360, 128], P('cell'), may hold values from 0.004 to 2, as said below
- h_factor: float32 [128, 16384], P('cell', 'gene'), may hold values from 0.03 to 0.3, as said below
Outputs:
- w_updated: float32 [15360, 128], P('cell')
- h_updated: float32 [128, 16384], P('cell', 'gene')
The draws below stay inside these ranges and needn't reach their ends.
Inputs may be any that keep to these rules, and one draw needn't show every extreme that they name: `counts`: nonnegative whole numbers. `w_factor`: positive. `h_factor`: positive.
All inputs are finite; a program needn't handle non-finite values.
Results may differ from the reference program's by a relative error of at most 0.00092.
Values may be sent and summed in bfloat16 or wider, within the bound.
No kernel may reach another device: no remote copies, remote signals or barrier semaphores. Data moves between devices by JAX's collectives and lax.ppermute only.
A program may use at most 64 MiB of HBM per device.

```python
import jax
import jax.numpy as jnp
from jax import lax

K = 128
GENES = 16384
CELL_DEV = 960
CELLS = 15360


def log_spread(key, shape, lower, upper):
    span = jnp.log(upper) - jnp.log(lower)
    return jnp.exp(jnp.log(lower) + span * jax.random.uniform(key, shape, jnp.float32))


def factor_pair(key):
    keys = jax.random.split(jax.random.fold_in(key, 101), 3)
    lower, upper, lift = (0.005, 0.05, 40.0)
    share = 4.0 / K
    base = log_spread(keys[0], (CELLS, K), lower, upper)
    raised = jnp.where(jax.random.uniform(keys[1], (CELLS, K), jnp.float32) < share, lift, 1.0)
    w_values = base * raised
    h_values = log_spread(keys[2], (K, GENES), 0.03, 0.3)
    return (w_values, h_values)


def draw_w_factor(key, part):
    w_values, h_values = factor_pair(key)
    return w_values


def draw_h_factor(key, part):
    w_values, h_values = factor_pair(key)
    return h_values


def draw_counts(key, part):
    w_values, h_values = factor_pair(key)
    keys = jax.random.split(jax.random.fold_in(key, 11), 4)
    tilt = log_spread(keys[0], (K, GENES), 0.3, 3.0)
    depth = log_spread(keys[1], (CELLS, 1), 0.3, 3.0)
    gene_scale = log_spread(keys[2], (1, GENES), 0.3, 3.0)
    expected = jnp.dot(w_values, h_values * tilt, precision=lax.Precision.HIGHEST)
    noise = jax.random.uniform(keys[3], (CELLS, GENES), jnp.float32)
    values = jnp.floor(3.0 * depth * gene_scale * noise * expected)
    values = jnp.minimum(values, 200.0)
    return values.astype(jnp.bfloat16)


def setup_inputs(seed: int = 0) -> dict:
    streams_of = jax.random.split(jax.random.key(seed), 4)
    counts = draw_counts(jax.random.fold_in(streams_of[3], 71), 0)
    w_factor = draw_w_factor(jax.random.fold_in(streams_of[3], 71), 0)
    h_factor = draw_h_factor(jax.random.fold_in(streams_of[3], 71), 0)
    return {"counts": counts, "w_factor": w_factor, "h_factor": h_factor}


def reference(counts, w_factor, h_factor):
    blocks = CELLS // CELL_DEV
    count_blocks = counts.reshape(blocks, CELL_DEV, GENES)
    w_blocks = w_factor.reshape(blocks, CELL_DEV, K)
    h_copy = h_factor.astype(jnp.bfloat16)

    def h_step(running, pair):
        block_counts, block_w = pair
        w_copy = block_w.astype(jnp.bfloat16)
        modeled = jnp.dot(w_copy, h_copy, preferred_element_type=jnp.float32)
        quotient = (block_counts.astype(jnp.float32) / modeled).astype(jnp.bfloat16)
        term = lax.dot_general(w_copy, quotient, (((0,), (0,)), ((), ())), preferred_element_type=jnp.float32)
        return running + term, None

    h_numerator, _ = lax.scan(h_step, jnp.zeros((K, GENES), jnp.float32), (count_blocks, w_blocks))
    w_totals = jnp.sum(w_factor, axis=0)
    h_updated = h_factor * h_numerator / w_totals[:, None]
    h_new_copy = h_updated.astype(jnp.bfloat16)
    h_totals = jnp.sum(h_new_copy.astype(jnp.float32), axis=1)

    def w_step(carry, pair):
        block_counts, block_w = pair
        w_copy = block_w.astype(jnp.bfloat16)
        modeled = jnp.dot(w_copy, h_new_copy, preferred_element_type=jnp.float32)
        quotient = (block_counts.astype(jnp.float32) / modeled).astype(jnp.bfloat16)
        numerator = lax.dot_general(quotient, h_new_copy, (((1,), (1,)), ((), ())), preferred_element_type=jnp.float32)
        return carry, block_w * numerator / h_totals[None, :]

    _, w_new = lax.scan(w_step, jnp.zeros((), jnp.float32), (count_blocks, w_blocks))
    return w_new.reshape(CELLS, K), h_updated
```

```python
import functools

import jax
import jax.numpy as jnp
from jax import lax
from jax.experimental import pallas as pl
from jax.experimental.pallas import tpu as pltpu
from jax.sharding import PartitionSpec as P

F32 = jnp.float32
BF16 = jnp.bfloat16
CHUNKS = 2
H_KNEE = 2.0**20
W_KNEE = 2.0**17


def encode(value, knee):
    part = jnp.minimum(value * (1.0 / knee), 1.0)
    return (value * part * part * part).astype(BF16)


def decode(code, knee):
    code = code.astype(F32)
    root = knee * jnp.sqrt(jnp.sqrt(code * (1.0 / knee)))
    return jnp.where(code < knee, root, code)


def h_kernel(offset, wt_ref, w_ref, *refs):
    pieces, counts_ref, out_ref = refs[:-2], refs[-2], refs[-1]
    h_tile = jnp.concatenate([piece[...] for piece in pieces], axis=0)
    modeled = jnp.dot(w_ref[...], h_tile, preferred_element_type=F32)
    quotient = (counts_ref[...].astype(F32) / modeled).astype(BF16)
    out_ref[...] = jnp.dot(wt_ref[...], quotient, preferred_element_type=F32)


def w_kernel(offset, w_ref, *refs, first):
    if first:
        pieces, counts_ref, out_ref, sum_ref = refs[:-3], refs[-3], refs[-2], refs[-1]
    else:
        pieces, counts_ref = refs[:-5], refs[-5]
        out_in, sum_in, out_ref, sum_ref = refs[-4:]
    h_tile = jnp.concatenate([piece[...] for piece in pieces], axis=0)
    across = (((1,), (1,)), ((), ()))
    ones = jnp.ones((sum_ref.shape[0], h_tile.shape[1]), BF16)

    @pl.when(pl.program_id(0) == 0)
    def _():
        if first:
            out_ref[...] = jnp.zeros_like(out_ref)
            sum_ref[...] = jnp.zeros_like(sum_ref)
        else:
            out_ref[...] = out_in[...]
            sum_ref[...] = sum_in[...]

    modeled = jnp.dot(w_ref[...], h_tile, preferred_element_type=F32)
    quotient = (counts_ref[...].astype(F32) / modeled).astype(BF16)
    out_ref[...] += lax.dot_general(quotient, h_tile, across, preferred_element_type=F32)
    sum_ref[...] += lax.dot_general(ones, h_tile, across, preferred_element_type=F32)


def tile_of(width):
    return next(t for t in (1024, 512, 256, 128, width) if width % t == 0)


def gene_specs(pieces, cells, width, tile):
    specs = [pl.BlockSpec((piece.shape[0], tile), lambda i, o: (0, i)) for piece in pieces]
    return specs + [pl.BlockSpec((cells, tile), lambda i, o: (0, o[0] + i))]


def cost(cells, rank, width):
    return pl.CostEstimate(
        flops=4 * cells * rank * width, transcendentals=0, bytes_accessed=2 * cells * width
    )


def h_partial(start, wt_rel, w_rel, pieces, counts, width):
    cells, rank = w_rel.shape
    tile = tile_of(width)
    return pl.pallas_call(
        h_kernel,
        grid_spec=pltpu.PrefetchScalarGridSpec(
            num_scalar_prefetch=1,
            grid=(width // tile,),
            in_specs=[
                pl.BlockSpec((rank, cells), lambda i, o: (0, 0)),
                pl.BlockSpec((cells, rank), lambda i, o: (0, 0)),
            ]
            + gene_specs(pieces, cells, width, tile),
            out_specs=pl.BlockSpec((rank, tile), lambda i, o: (0, i)),
        ),
        out_shape=jax.ShapeDtypeStruct((rank, width), F32),
        cost_estimate=cost(cells, rank, width),
        name="h_partial",
    )((start // tile)[None], wt_rel, w_rel, *pieces, counts)


def w_partial(start, w_rel, pieces, counts, width, running):
    cells, rank = w_rel.shape
    tile = tile_of(width)
    whole = [
        pl.BlockSpec((cells, rank), lambda i, o: (0, 0)),
        pl.BlockSpec((8, rank), lambda i, o: (0, 0)),
    ]
    first = running is None
    extra = () if first else running
    aliases = {} if first else {3 + len(pieces): 0, 4 + len(pieces): 1}
    return pl.pallas_call(
        functools.partial(w_kernel, first=first),
        grid_spec=pltpu.PrefetchScalarGridSpec(
            num_scalar_prefetch=1,
            grid=(width // tile,),
            in_specs=[pl.BlockSpec((cells, rank), lambda i, o: (0, 0))]
            + gene_specs(pieces, cells, width, tile)
            + ([] if first else whole),
            out_specs=whole,
        ),
        out_shape=[
            jax.ShapeDtypeStruct((cells, rank), F32),
            jax.ShapeDtypeStruct((8, rank), F32),
        ],
        input_output_aliases=aliases,
        cost_estimate=cost(cells, rank, width),
        name="w_partial",
    )((start // tile)[None], w_rel, *pieces, counts, *extra)


def per_device(counts, w_factor, h_factor, *, devices, gene_devices):
    own_rows, genes = h_factor.shape
    cells, rank = w_factor.shape
    chips = devices // 2
    across = 2 ** ((chips.bit_length() - 1) // 2)
    along = chips // across
    rows = 2 * own_rows
    half = genes // 2
    width = half // CHUNKS

    index = lax.axis_index("cell")
    core = index % 2
    x_at = (index // 2) % across
    z_at = index // (2 * across)

    def send(value, route):
        return lax.ppermute(value, "cell", [(i, route(i)) for i in range(devices)])

    def swap(value):
        return send(value, lambda i: i ^ 1)

    def shift_x(value, s):
        return send(
            value, lambda i: i % 2 + 2 * ((i // 2 + s) % across) + i // (2 * across) * 2 * across
        )

    def shift_z(value, s):
        return send(value, lambda i: (i + 2 * across * s) % devices)

    place = jnp.arange(rank)
    source = (
        (z_at + place // rows % along) % along * (across * rows)
        + (x_at + place // (rows * along)) % across * rows
        + place % rows
    )
    pick = source[:, None] == jnp.arange(rank)[None, :]

    w_copy = w_factor.astype(BF16)
    w_rel = lax.dot_general(
        w_copy, pick.astype(BF16), (((1,), (1,)), ((), ())), preferred_element_type=F32
    ).astype(BF16)
    wt_rel = lax.dot_general(
        pick.astype(BF16), w_copy, (((1,), (1,)), ((), ())), preferred_element_type=F32
    ).astype(BF16)

    own_half = lax.dynamic_slice_in_dim(h_factor, core * half, half, 1)
    other_half = lax.dynamic_slice_in_dim(h_factor, (1 - core) * half, half, 1)
    w_sum = jnp.broadcast_to(jnp.sum(w_factor, axis=0)[None, :], (8, rank))
    got_half = swap(other_half)
    w_sum = (w_sum + swap(w_sum))[0]
    h_chip = jnp.where(
        core == 0,
        jnp.concatenate([own_half, got_half], 0),
        jnp.concatenate([got_half, own_half], 0),
    )
    h_chip_copy = h_chip.astype(BF16)
    high = lax.reduce_precision(w_sum, 8, 7)
    middle = lax.reduce_precision(w_sum - high, 8, 7)
    low = w_sum - high - middle
    sums = jnp.concatenate(
        [jnp.stack([high, middle, low]), jnp.zeros((rows - 3, rank), F32)], 0
    ).astype(BF16)

    def gather(block):
        column = jnp.concatenate(
            [block] + [shift_z(block, along - s) for s in range(1, along)], 0
        )
        own = [column] + [shift_x(column, across - s) for s in range(1, across)]
        return own, [swap(piece) for piece in own]

    def reduce(own, other):
        total = own + swap(other)
        block = along * rows
        sent = encode(total[block:], H_KNEE)
        column = total[:block]
        for s in range(1, across):
            column = column + decode(shift_x(sent[(s - 1) * block : s * block], s), H_KNEE)
        sent = encode(column[rows:], H_KNEE)
        mine = column[:rows]
        for s in range(1, along):
            mine = mine + decode(shift_z(sent[(s - 1) * rows : s * rows], s), H_KNEE)
        return mine

    starts = []
    for i in range(CHUNKS):
        starts.append((core * half + i * width, (1 - core) * half + i * width))

    gathered = []
    for i in range(CHUNKS):
        block = h_chip_copy[:, i * width : (i + 1) * width]
        if i == 0:
            block = jnp.concatenate([block, sums], 1)
        gathered.append(gather(block))
    w_totals = sum(jnp.sum(piece[:, width:].astype(F32), axis=0) for piece in gathered[0][0])
    own_totals = lax.dynamic_slice_in_dim(w_totals, index // 2 * rows, rows, 0)[:, None]

    updated = []
    again = []
    for i in range(CHUNKS):
        own, other = gathered[i]
        for_other = h_partial(starts[i][1], wt_rel, w_rel, other, counts, width)
        for_own = h_partial(starts[i][0], wt_rel, w_rel, own, counts, width)
        numerator = reduce(for_own, for_other)
        new = h_chip[:, i * width : (i + 1) * width] * numerator / own_totals
        updated.append(new)
        again.append(gather(new.astype(BF16)))

    running = None
    for i in range(CHUNKS):
        own, other = again[i]
        running = w_partial(starts[i][0], w_rel, own, counts, width, running)
        running = w_partial(starts[i][1], w_rel, other, counts, width, running)

    new = jnp.concatenate(updated, 1)
    kept = lax.dynamic_slice_in_dim(new, core * own_rows, own_rows, 0)
    got = swap(lax.dynamic_slice_in_dim(new, (1 - core) * own_rows, own_rows, 0))
    h_updated = jnp.where(
        core == 0, jnp.concatenate([kept, got], 1), jnp.concatenate([got, kept], 1)
    )

    w_numerator, h_totals = running
    if gene_devices == 2:
        swap_gene = [(0, 1), (1, 0)]
        code = encode(w_numerator, W_KNEE)
        got_code = lax.ppermute(code, "gene", swap_gene)
        h_totals = h_totals + lax.ppermute(h_totals, "gene", swap_gene)
        w_numerator = decode(code, W_KNEE) + decode(got_code, W_KNEE)
    else:
        w_numerator, h_totals = lax.psum((w_numerator, h_totals), "gene")
    ratio = w_numerator / h_totals[:1]
    ratio = jnp.dot(ratio, pick.astype(F32), precision=lax.Precision.HIGHEST)
    return (w_factor * ratio, h_updated)


def solution(mesh):
    in_specs = (P("cell", "gene"), P("cell", None), P("cell", "gene"))
    out_specs = (P("cell", None), P("cell", "gene"))
    body = functools.partial(
        per_device, devices=mesh.shape["cell"], gene_devices=mesh.shape["gene"]
    )
    return jax.shard_map(
        body, mesh=mesh, in_specs=in_specs, out_specs=out_specs, check_vma=False
    )
```

```python
import functools

import jax
import jax.numpy as jnp
from jax import lax
from jax.experimental import pallas as pl
from jax.experimental.pallas import tpu as pltpu
from jax.sharding import PartitionSpec as P


F32 = jnp.float32
BF16 = jnp.bfloat16
CHUNKS = 2
H_KNEE = 2.0**20
W_KNEE = 2.0**17


def encode(value, knee):
    part = jnp.minimum(value * (1.0 / knee), 1.0)
    return (value * part * part * part).astype(BF16)


def decode(code, knee):
    code = code.astype(F32)
    root = knee * jnp.sqrt(jnp.sqrt(code * (1.0 / knee)))
    return jnp.where(code < knee, root, code)


def prepare_kernel(w_ref, pick_ref, w_rel_ref, wt_rel_ref, sum_ref):
    w_value = w_ref[...]
    w_copy = w_value.astype(BF16)
    pick = pick_ref[...]
    second = (((1,), (1,)), ((), ()))
    w_rel_ref[...] = lax.dot_general(w_copy, pick, second, preferred_element_type=F32).astype(BF16)
    wt_rel_ref[...] = lax.dot_general(pick, w_copy, second, preferred_element_type=F32).astype(BF16)
    sum_ref[...] = jnp.broadcast_to(jnp.sum(w_value, axis=0, keepdims=True), sum_ref.shape)


def prepare(w_factor, pick):
    cells, rank = w_factor.shape
    return pl.pallas_call(
        prepare_kernel,
        out_shape=[
            jax.ShapeDtypeStruct((cells, rank), BF16),
            jax.ShapeDtypeStruct((rank, cells), BF16),
            jax.ShapeDtypeStruct((8, rank), F32),
        ],
        name="prepare",
    )(w_factor, pick)


def h_kernel(wt_ref, w_ref, *refs):
    pieces, counts_ref, keep_ref, send_ref = refs[:-3], refs[-3], refs[-2], refs[-1]
    h_tile = jnp.concatenate([piece[...] for piece in pieces], axis=0)
    modeled = jnp.dot(w_ref[...], h_tile, preferred_element_type=F32)
    quotient = (counts_ref[...].astype(F32) / modeled).astype(BF16)
    term = jnp.dot(wt_ref[...], quotient, preferred_element_type=F32)
    keep = keep_ref.shape[0]
    keep_ref[...] = term[:keep]
    send_ref[...] = term[keep:]


def w_kernel(w_ref, *refs, count, first, last):
    pieces, counts_ref = refs[:count], refs[count]
    running = refs[count + 1 : -3]
    out_ref, sum_ref, total_ref = refs[-3:]
    h_tile = jnp.concatenate([piece[...] for piece in pieces], axis=0)
    across = (((1,), (1,)), ((), ()))
    ones = jnp.ones((sum_ref.shape[0], h_tile.shape[1]), BF16)

    @pl.when(pl.program_id(0) == 0)
    def _():
        if first:
            total_ref[...] = jnp.zeros_like(total_ref)
            sum_ref[...] = jnp.zeros_like(sum_ref)
        else:
            total_ref[...] = running[0][...]
            sum_ref[...] = running[1][...]

    modeled = jnp.dot(w_ref[...], h_tile, preferred_element_type=F32)
    quotient = (counts_ref[...].astype(F32) / modeled).astype(BF16)
    total_ref[...] += lax.dot_general(quotient, h_tile, across, preferred_element_type=F32)
    sum_ref[...] += lax.dot_general(ones, h_tile, across, preferred_element_type=F32)

    @pl.when(pl.program_id(0) == pl.num_programs(0) - 1)
    def _():
        total = total_ref[...]
        out_ref[...] = encode(total, W_KNEE) if last else total


def tile_of(width):
    return next(t for t in (1024, 512, 256, 128, width) if width % t == 0)


def cost(cells, rank, width):
    return pl.CostEstimate(
        flops=4 * cells * rank * width, transcendentals=0, bytes_accessed=2 * cells * width
    )


def h_partial(start, wt_rel, w_rel, pieces, counts, width):
    cells, rank = w_rel.shape
    tile = tile_of(width)
    part = pl.BlockSpec((rank // 2, tile), lambda i: (0, i))
    return pl.pallas_call(
        h_kernel,
        grid=(width // tile,),
        in_specs=[
            pl.BlockSpec((rank, cells), lambda i: (0, 0)),
            pl.BlockSpec((cells, rank), lambda i: (0, 0)),
        ]
        + [pl.BlockSpec((piece.shape[0], tile), lambda i: (0, i)) for piece in pieces]
        + [pl.BlockSpec((cells, tile), lambda i: (0, start // tile + i))],
        out_specs=[part, part],
        out_shape=[jax.ShapeDtypeStruct((rank // 2, width), F32)] * 2,
        cost_estimate=cost(cells, rank, width),
        name="h_partial",
    )(wt_rel, w_rel, *pieces, counts)


def w_partial(start, w_rel, pieces, counts, width, running, last):
    cells, rank = w_rel.shape
    tile = tile_of(width)
    rows = pl.BlockSpec((cells, rank), lambda i: (0, 0))
    sums = pl.BlockSpec((8, rank), lambda i: (0, 0))
    return pl.pallas_call(
        functools.partial(w_kernel, count=len(pieces), first=not running, last=last),
        grid=(width // tile,),
        in_specs=[rows]
        + [pl.BlockSpec((piece.shape[0], tile), lambda i: (0, i)) for piece in pieces]
        + [pl.BlockSpec((cells, tile), lambda i: (0, start // tile + i))]
        + ([rows, sums] if running else []),
        out_specs=[rows, sums],
        scratch_shapes=[pltpu.VMEM((cells, rank), F32)],
        out_shape=[
            jax.ShapeDtypeStruct((cells, rank), BF16 if last else F32),
            jax.ShapeDtypeStruct((8, rank), F32),
        ],
        cost_estimate=cost(cells, rank, width),
        name="w_partial",
    )(w_rel, *pieces, counts, *running)


def per_device(counts, w_factor, h_factor, *, devices, gene_devices):
    rows, genes = h_factor.shape
    _, rank = w_factor.shape
    chips = devices // 2
    across = 2 ** ((chips.bit_length() - 1) // 2)
    along = chips // across
    block = along * rows
    width = genes // CHUNKS

    index = lax.axis_index("cell")
    core = index % 2
    x_at = (index // 2) % across
    z_at = index // (2 * across)

    def send(value, route):
        return lax.ppermute(value, "cell", [(i, route(i)) for i in range(devices)])

    def swap(value):
        return send(value, lambda i: i ^ 1)

    def shift_x(value, s):
        return send(
            value, lambda i: i % 2 + 2 * ((i // 2 + s) % across) + i // (2 * across) * 2 * across
        )

    def shift_z(value, s):
        return send(value, lambda i: (i + 2 * across * s) % devices)

    place = jnp.arange(rank)
    source = (
        (z_at + place // rows % along) % along * (2 * across * rows)
        + (x_at + place // block % across) % across * (2 * rows)
        + (core + place // (block * across)) % 2 * rows
        + place % rows
    )
    pick = source[:, None] == jnp.arange(rank)[None, :]

    w_rel, wt_rel, w_sum = prepare(w_factor, pick.astype(BF16))
    w_sum = w_sum[0]
    high = lax.reduce_precision(w_sum, 8, 7)
    middle = lax.reduce_precision(w_sum - high, 8, 7)
    low = w_sum - high - middle
    lanes = -(-3 // rows)
    sums = jnp.pad(jnp.stack([high, middle, low]), ((0, lanes * rows - 3), (0, 0)))
    sums = jnp.concatenate(jnp.split(sums, lanes, 0), 1).astype(BF16)

    def gather(own):
        column = [own] + [shift_z(own, along - s) for s in range(1, along)]
        column = jnp.concatenate(column, 0)
        mine = [column] + [shift_x(column, across - s) for s in range(1, across)]
        return mine + [swap(piece) for piece in mine]

    def reduce(keep, other):
        total = keep + swap(other)
        sent = encode(total[block:], H_KNEE)
        column = total[:block]
        got = [shift_x(sent[(s - 1) * block : s * block], s) for s in range(1, across)]
        for piece in got:
            column = column + decode(piece, H_KNEE)
        sent = encode(column[rows:], H_KNEE)
        mine = column[:rows]
        got = [shift_z(sent[(s - 1) * rows : s * rows], s) for s in range(1, along)]
        for piece in got:
            mine = mine + decode(piece, H_KNEE)
        return mine

    gathered = []
    for i in range(CHUNKS):
        own = h_factor[:, i * width : (i + 1) * width].astype(BF16)
        if i == CHUNKS - 1:
            own = jnp.concatenate([own, sums], 1)
        gathered.append(gather(own))
    w_totals = jnp.concatenate([piece[:, width:] for piece in gathered[-1]], 0).astype(F32)
    w_totals = jnp.sum(jnp.sum(w_totals, axis=0).reshape(lanes, rank), axis=0)
    own_totals = lax.dynamic_slice_in_dim(w_totals, index * rows, rows, 0)[:, None]

    updated = []
    again = []
    for i in range(CHUNKS):
        keep, other = h_partial(i * width, wt_rel, w_rel, gathered[i], counts, width)
        numerator = reduce(keep, other)
        if updated:
            numerator, _ = lax.optimization_barrier((numerator, updated[-1]))
        new = h_factor[:, i * width : (i + 1) * width] * numerator / own_totals
        updated.append(new)
        again.append(gather(new.astype(BF16)))
    h_updated = jnp.concatenate(updated, 1)

    running = ()
    for i in range(CHUNKS):
        last = i == CHUNKS - 1 and gene_devices == 2
        running = w_partial(i * width, w_rel, again[i], counts, width, running, last)
    numerator, h_totals = running

    if gene_devices == 2:
        swap_gene = [(0, 1), (1, 0)]
        h_totals = h_totals + lax.ppermute(h_totals, "gene", swap_gene)
        got = lax.ppermute(numerator, "gene", swap_gene)
        numerator = decode(numerator, W_KNEE) + decode(got, W_KNEE)
    else:
        numerator, h_totals = lax.psum((numerator, h_totals), "gene")
    ratio = jnp.dot(
        numerator / h_totals[:1], pick.astype(F32), precision=lax.Precision.HIGHEST
    )
    w_updated = w_factor * ratio
    return (w_updated, h_updated)


def solution(mesh):
    in_specs = (P("cell", "gene"), P("cell", None), P("cell", "gene"))
    out_specs = (P("cell", None), P("cell", "gene"))

    def body(counts, w_factor, h_factor):
        return per_device(
            counts,
            w_factor,
            h_factor,
            devices=mesh.shape["cell"],
            gene_devices=mesh.shape["gene"],
        )

    return jax.shard_map(
        body, mesh=mesh, in_specs=in_specs, out_specs=out_specs, check_vma=False
    )
```

```python
import functools
import math

import jax
import jax.numpy as jnp
from jax import lax
from jax.experimental import pallas as pl
from jax.experimental.pallas import tpu as pltpu
from jax.sharding import PartitionSpec as P


F32 = jnp.float32
BF16 = jnp.bfloat16
SPACE = pltpu.VMEM
SPLIT = (4, 4)
H_KNEE = 2.0**20
W_KNEE = 2.0**17


def encode(value, knee):
    part = jnp.minimum(value * (1.0 / knee), 1.0)
    return (value * part * part * part).astype(BF16)


def decode(code, knee):
    code = code.astype(F32)
    root = knee * lax.rsqrt(lax.rsqrt(code * (1.0 / knee)))
    return jnp.where(code < knee, root, code)


def encode_square(value, knee):
    return (value * jnp.minimum(value * (1.0 / knee), 1.0)).astype(BF16)


def decode_square(code, knee):
    code = code.astype(F32)
    square = code * knee
    return jnp.where(code < knee, square * lax.rsqrt(jnp.maximum(square, 1e-30)), code)


def prepare_kernel(w_ref, pick_ref, w_rel_ref, wt_rel_ref, sum_ref):
    w_value = w_ref[...]
    w_copy = w_value.astype(BF16)
    pick = pick_ref[...]
    second = (((1,), (1,)), ((), ()))
    w_rel_ref[...] = lax.dot_general(w_copy, pick, second, preferred_element_type=F32).astype(BF16)
    wt_rel_ref[...] = lax.dot_general(pick, w_copy, second, preferred_element_type=F32).astype(BF16)
    sum_ref[...] = jnp.broadcast_to(jnp.sum(w_value, axis=0, keepdims=True), sum_ref.shape)


def prepare(w_factor, pick):
    cells, rank = w_factor.shape
    return pl.pallas_call(
        prepare_kernel,
        out_shape=[
            jax.ShapeDtypeStruct((cells, rank), BF16),
            jax.ShapeDtypeStruct((rank, cells), BF16),
            jax.ShapeDtypeStruct((8, rank), F32),
        ],
        name="prepare",
    )(w_factor, pick)


def h_kernel(wt_ref, w_ref, *refs):
    pieces, counts_ref, keep_ref, send_ref = refs[:-3], refs[-3], refs[-2], refs[-1]
    h_tile = jnp.concatenate([piece[...] for piece in pieces], axis=0)
    modeled = jnp.dot(w_ref[...], h_tile, preferred_element_type=F32)
    quotient = (counts_ref[...].astype(F32) / modeled).astype(BF16)
    term = jnp.dot(wt_ref[...], quotient, preferred_element_type=F32)
    keep = keep_ref.shape[0]
    keep_ref[...] = term[:keep]
    send_ref[...] = encode_square(term[keep:], H_KNEE)


def w_kernel(w_ref, *refs, count, first, last):
    pieces, counts_ref = refs[:count], refs[count]
    if last:
        running, pick_ref = refs[count + 1 : -4], refs[-4]
        out_ref, total_ref, sum_ref = refs[-3:]
    else:
        running = refs[count + 1 : -2]
        total_ref, sum_ref = refs[-2:]
    h_tile = jnp.concatenate([piece[...] for piece in pieces], axis=0)
    across = (((1,), (1,)), ((), ()))
    ones = jnp.ones((sum_ref.shape[0], h_tile.shape[1]), BF16)

    @pl.when(pl.program_id(0) == 0)
    def _():
        if first:
            total_ref[...] = jnp.zeros_like(total_ref)
            sum_ref[...] = jnp.zeros_like(sum_ref)
        else:
            total_ref[...] = running[0][...]
            sum_ref[...] = running[1][...]

    modeled = jnp.dot(w_ref[...], h_tile, preferred_element_type=F32)
    quotient = (counts_ref[...].astype(F32) / modeled).astype(BF16)
    total_ref[...] += lax.dot_general(quotient, h_tile, across, preferred_element_type=F32)
    sum_ref[...] += lax.dot_general(ones, h_tile, across, preferred_element_type=F32)

    if last:

        @pl.when(pl.program_id(0) == pl.num_programs(0) - 1)
        def _():
            cells = total_ref.shape[0]
            exact = lax.Precision.HIGHEST
            pick = pick_ref[...]
            total = jnp.dot(total_ref[...], pick, precision=exact, preferred_element_type=F32)
            sums = jnp.dot(sum_ref[...], pick, precision=exact, preferred_element_type=F32)
            high = sums.astype(BF16)
            rest = sums - high.astype(F32)
            middle = rest.astype(BF16)
            low = (rest - middle.astype(F32)).astype(BF16)
            out_ref[:cells, :] = encode(total, W_KNEE)
            row = lax.broadcasted_iota(jnp.int32, (16, sums.shape[1]), 0)
            part = [jnp.broadcast_to(x.astype(F32)[:1], row.shape) for x in (high, middle, low)]
            tail = jnp.where(row == 0, part[0], jnp.where(row == 1, part[1], part[2]))
            out_ref[cells:, :] = jnp.where(row < 3, tail, 0.0).astype(BF16)


def tile_of(width):
    return next(t for t in (2048, 1024, 512, 256, 128, width) if width % t == 0)


def cost(cells, rank, width):
    return pl.CostEstimate(
        flops=4 * cells * rank * width, transcendentals=0, bytes_accessed=2 * cells * width
    )


def held(pieces):
    return [pltpu.with_memory_space_constraint(piece, SPACE) for piece in pieces]


def h_partial(start, wt_rel, w_rel, pieces, counts, width):
    cells, rank = w_rel.shape
    tile = tile_of(math.gcd(width, start))
    part = pl.BlockSpec((rank // 2, tile), lambda i: (0, i))
    return pl.pallas_call(
        h_kernel,
        grid=(width // tile,),
        in_specs=[
            pl.BlockSpec((rank, cells), lambda i: (0, 0)),
            pl.BlockSpec((cells, rank), lambda i: (0, 0)),
        ]
        + [pl.BlockSpec((piece.shape[0], tile), lambda i: (0, i)) for piece in pieces]
        + [pl.BlockSpec((cells, tile), lambda i: (0, start // tile + i))],
        out_specs=[part, part],
        out_shape=[jax.ShapeDtypeStruct((rank // 2, width), kind) for kind in (F32, BF16)],
        cost_estimate=cost(cells, rank, width),
        name="h_partial",
    )(wt_rel, w_rel, *held(pieces), counts)


def w_partial(start, w_rel, pieces, counts, width, running, pick):
    cells, rank = w_rel.shape
    tile = tile_of(math.gcd(width, start))
    last = pick is not None
    rows = pl.BlockSpec((cells, rank), lambda i: (0, 0))
    sums = pl.BlockSpec((8, rank), lambda i: (0, 0))
    square = pl.BlockSpec((rank, rank), lambda i: (0, 0))
    if last:
        how = dict(
            out_specs=pl.BlockSpec((cells + 16, rank), lambda i: (0, 0)),
            out_shape=jax.ShapeDtypeStruct((cells + 16, rank), BF16),
            scratch_shapes=[pltpu.VMEM((cells, rank), F32), pltpu.VMEM((8, rank), F32)],
        )
    else:
        how = dict(
            out_specs=[rows, sums],
            out_shape=[
                jax.ShapeDtypeStruct((cells, rank), F32),
                jax.ShapeDtypeStruct((8, rank), F32),
            ],
        )
    return pl.pallas_call(
        functools.partial(w_kernel, count=len(pieces), first=not running, last=last),
        grid=(width // tile,),
        in_specs=[rows]
        + [pl.BlockSpec((piece.shape[0], tile), lambda i: (0, i)) for piece in pieces]
        + [pl.BlockSpec((cells, tile), lambda i: (0, start // tile + i))]
        + ([rows, sums] if running else [])
        + ([square] if last else []),
        cost_estimate=cost(cells, rank, width),
        name="w_partial",
        **how,
    )(w_rel, *held(pieces), counts, *running, *([pick] if last else []))


def per_device(counts, w_factor, h_factor, *, devices, gene_devices):
    rows, genes = h_factor.shape
    cells, rank = w_factor.shape
    chips = devices // 2
    across = 2 ** ((chips.bit_length() - 1) // 2)
    along = chips // across
    block = along * rows
    widths = [genes * share // sum(SPLIT) for share in SPLIT]
    starts = [sum(widths[:i]) for i in range(len(widths))]
    chunks = len(widths)

    index = lax.axis_index("cell")
    core = index % 2
    x_at = (index // 2) % across
    z_at = index // (2 * across)

    def send(value, route):
        return lax.ppermute(value, "cell", [(i, route(i)) for i in range(devices)])

    def swap(value):
        return send(value, lambda i: i ^ 1)

    def shift_x(value, s):
        return send(
            value, lambda i: i % 2 + 2 * ((i // 2 + s) % across) + i // (2 * across) * 2 * across
        )

    def shift_z(value, s):
        return send(value, lambda i: (i + 2 * across * s) % devices)

    place = jnp.arange(rank)
    source = (
        (z_at + place // rows % along) % along * (2 * across * rows)
        + (x_at + place // block % across) % across * (2 * rows)
        + (core + place // (block * across)) % 2 * rows
        + place % rows
    )
    pick = source[:, None] == jnp.arange(rank)[None, :]

    w_rel, wt_rel, w_sum = prepare(w_factor, pick.astype(BF16))
    w_sum = w_sum[0]
    high = lax.reduce_precision(w_sum, 8, 7)
    middle = lax.reduce_precision(w_sum - high, 8, 7)
    low = w_sum - high - middle
    lanes = -(-3 // rows)
    sums = jnp.pad(jnp.stack([high, middle, low]), ((0, lanes * rows - 3), (0, 0)))
    sums = jnp.concatenate(jnp.split(sums, lanes, 0), 1).astype(BF16)

    def gather(own):
        column = [own]
        for s in range(1, along):
            column.append(shift_z(own, along - s))
        column = jnp.concatenate(column, 0)
        mine = [column] + [shift_x(column, across - s) for s in range(1, across)]
        return mine + [swap(piece) for piece in mine]

    def reduce(keep, other):
        total = keep + decode_square(swap(other), H_KNEE)
        sent = encode(total[block:], H_KNEE)
        column = total[:block]
        got = [shift_x(sent[(s - 1) * block : s * block], s) for s in range(1, across)]
        for piece in got:
            column = column + decode(piece, H_KNEE)
        sent = encode(column[rows:], H_KNEE)
        mine = column[:rows]
        got = []
        for s in range(1, along):
            got.append(shift_z(sent[(s - 1) * rows : s * rows], s))
        for piece in got:
            mine = mine + decode(piece, H_KNEE)
        return mine

    gathered = []
    for i in range(chunks):
        own = h_factor[:, starts[i] : starts[i] + widths[i]].astype(BF16)
        if i == chunks - 1:
            own = jnp.concatenate([own, sums], 1)
        gathered.append(gather(own))
    w_totals = jnp.concatenate([piece[:, widths[-1] :] for piece in gathered[-1]], 0).astype(F32)
    w_totals = jnp.sum(jnp.sum(w_totals, axis=0).reshape(lanes, rank), axis=0)
    own_totals = lax.dynamic_slice_in_dim(w_totals, index * rows, rows, 0)[:, None]

    updated = []
    again = []
    for i in range(chunks):
        keep, other = h_partial(starts[i], wt_rel, w_rel, gathered[i], counts, widths[i])
        numerator = reduce(keep, other)
        if updated:
            numerator, _ = lax.optimization_barrier((numerator, updated[-1]))
        new = h_factor[:, starts[i] : starts[i] + widths[i]] * numerator / own_totals
        updated.append(new)
        again.append(gather(new.astype(BF16)))
    h_updated = jnp.concatenate(updated, 1)

    pick = pick.astype(F32)
    running = ()
    for i in range(chunks):
        last = i == chunks - 1 and gene_devices == 2
        running = w_partial(
            starts[i], w_rel, again[i], counts, widths[i], running, pick if last else None
        )
    if gene_devices == 2:
        got = lax.ppermute(running, "gene", [(0, 1), (1, 0)])
        totals = sum(
            side[cells + row : cells + row + 1].astype(F32)
            for row in range(3)
            for side in (running, got)
        )
        numerator = decode(running[:cells], W_KNEE) + decode(got[:cells], W_KNEE)
        w_updated = w_factor * numerator / totals
    else:
        numerator, h_totals = lax.psum(running, "gene")
        ratio = jnp.dot(numerator / h_totals[:1], pick, precision=lax.Precision.HIGHEST)
        w_updated = w_factor * ratio
    return (w_updated, h_updated)


def solution(mesh):
    in_specs = (P("cell", "gene"), P("cell", None), P("cell", "gene"))
    out_specs = (P("cell", None), P("cell", "gene"))

    def body(counts, w_factor, h_factor):
        return per_device(
            counts,
            w_factor,
            h_factor,
            devices=mesh.shape["cell"],
            gene_devices=mesh.shape["gene"],
        )

    return jax.shard_map(
        body, mesh=mesh, in_specs=in_specs, out_specs=out_specs, check_vma=False
    )
```

```python
import functools

import jax
import jax.numpy as jnp
from jax import lax
from jax.experimental import pallas as pl
from jax.experimental.pallas import tpu as pltpu
from jax.sharding import PartitionSpec as P


F32 = jnp.float32
BF16 = jnp.bfloat16
SPACE = pltpu.VMEM
H_SHARES = (1, 1, 2, 4)
W_SHARES = (1, 1, 1, 1)
LIMIT = 40 << 20
SPLIT = (4, 4)
H_KNEE = 2.0**20
W_KNEE = 2.0**17


def encode(value, knee):
    part = jnp.minimum(value * (1.0 / knee), 1.0)
    return (value * part * part * part).astype(BF16)


def decode(code, knee):
    code = code.astype(F32)
    root = knee * lax.rsqrt(lax.rsqrt(code * (1.0 / knee)))
    return jnp.where(code < knee, root, code)


def encode_square(value, knee):
    return (value * jnp.minimum(value * (1.0 / knee), 1.0)).astype(BF16)


def decode_square(code, knee):
    code = code.astype(F32)
    square = code * knee
    return jnp.where(code < knee, square * lax.rsqrt(jnp.maximum(square, 1e-30)), code)


def parts_of(value):
    high = value.astype(BF16)
    rest = value - high.astype(F32)
    middle = rest.astype(BF16)
    low = (rest - middle.astype(F32)).astype(BF16)
    return [part.astype(F32) for part in (high, middle, low)]


def prepare_kernel(w_ref, pick_ref, w_rel_ref, wt_rel_ref, sum_ref):
    w_value = w_ref[...]
    w_copy = w_value.astype(BF16)
    pick = pick_ref[...]
    second = (((1,), (1,)), ((), ()))
    w_rel_ref[...] = lax.dot_general(w_copy, pick, second, preferred_element_type=F32).astype(BF16)
    wt_rel_ref[...] = lax.dot_general(pick, w_copy, second, preferred_element_type=F32).astype(BF16)
    rank = w_ref.shape[1]
    rows = sum_ref.shape[0]
    high, middle, low = parts_of(jnp.sum(w_value, axis=0, keepdims=True))
    for block in range(sum_ref.shape[1] // rank):
        row = lax.broadcasted_iota(jnp.int32, (rows, rank), 0) + block * rows
        value = jnp.where(row == 0, high, jnp.where(row == 1, middle, low))
        sum_ref[:, block * rank : (block + 1) * rank] = jnp.where(row < 3, value, 0.0).astype(BF16)


def prepare(w_factor, pick, sum_shape):
    cells, rank = w_factor.shape
    return pl.pallas_call(
        prepare_kernel,
        out_shape=[
            jax.ShapeDtypeStruct((cells, rank), BF16),
            jax.ShapeDtypeStruct((rank, cells), BF16),
            jax.ShapeDtypeStruct(sum_shape, BF16),
        ],
        compiler_params=pltpu.CompilerParams(vmem_limit_bytes=LIMIT),
        name="prepare",
    )(w_factor, pick)


def streamed(counts_ref, buffer_ref, sems, start, shares):
    width = buffer_ref.shape[1]
    sizes = [width * share // sum(shares) for share in shares]
    copies = []
    at = 0
    for i, size in enumerate(sizes):
        copy = pltpu.make_async_copy(
            counts_ref.at[:, pl.ds(start + at, size)],
            buffer_ref.at[:, pl.ds(at, size)],
            sems.at[i],
        )
        copy.start()
        copies.append((copy, slice(at, at + size)))
        at += size
    return copies


def quotient_of(w_ref, h_tile, block):
    modeled = jnp.dot(w_ref[...], h_tile, preferred_element_type=F32)
    return (block.astype(F32) / modeled).astype(BF16)


def h_kernel(wt_ref, w_ref, *refs, start):
    pieces, (counts_ref, keep_ref, send_ref, buffer_ref, sems) = refs[:-5], refs[-5:]
    keep = keep_ref.shape[0]
    for copy, span in streamed(counts_ref, buffer_ref, sems, start, H_SHARES):
        h_tile = jnp.concatenate([piece[:, span] for piece in pieces], axis=0)
        copy.wait()
        quotient = quotient_of(w_ref, h_tile, buffer_ref[:, span])
        term = jnp.dot(wt_ref[...], quotient, preferred_element_type=F32)
        keep_ref[:, span] = term[:keep]
        send_ref[:, span] = encode_square(term[keep:], H_KNEE)


def w_kernel(w_ref, *refs, count, start, first, last):
    pieces, counts_ref = refs[:count], refs[count]
    if last:
        running, pick_ref = refs[count + 1 : -6], refs[-6]
        out_ref, buffer_ref, sems, total_ref, sum_ref = refs[-5:]
    else:
        running = refs[count + 1 : -4]
        total_ref, sum_ref, buffer_ref, sems = refs[-4:]
    copies = streamed(counts_ref, buffer_ref, sems, start, W_SHARES)
    across = (((1,), (1,)), ((), ()))
    if first:
        total_ref[...] = jnp.zeros_like(total_ref)
        sum_ref[...] = jnp.zeros_like(sum_ref)
    else:
        total_ref[...] = running[0][...]
        sum_ref[...] = running[1][...]
    for copy, span in copies:
        h_tile = jnp.concatenate([piece[:, span] for piece in pieces], axis=0)
        ones = jnp.ones((sum_ref.shape[0], h_tile.shape[1]), BF16)
        copy.wait()
        quotient = quotient_of(w_ref, h_tile, buffer_ref[:, span])
        total_ref[...] += lax.dot_general(quotient, h_tile, across, preferred_element_type=F32)
        sum_ref[...] += lax.dot_general(ones, h_tile, across, preferred_element_type=F32)

    if last:
        cells = total_ref.shape[0]
        exact = lax.Precision.HIGHEST
        pick = pick_ref[...]
        total = jnp.dot(total_ref[...], pick, precision=exact, preferred_element_type=F32)
        sums = jnp.dot(sum_ref[...], pick, precision=exact, preferred_element_type=F32)
        high, middle, low = parts_of(sums[:1])
        out_ref[:cells, :] = encode(total, W_KNEE)
        row = lax.broadcasted_iota(jnp.int32, (16, sums.shape[1]), 0)
        tail = jnp.where(row == 0, high, jnp.where(row == 1, middle, low))
        out_ref[cells:, :] = jnp.where(row < 3, tail, 0.0).astype(BF16)


def cost(cells, rank, width):
    return pl.CostEstimate(
        flops=4 * cells * rank * width, transcendentals=0, bytes_accessed=2 * cells * width
    )


def held(pieces):
    return [pltpu.with_memory_space_constraint(piece, SPACE) for piece in pieces]


def call(kernel, held_args, counts, more_args, outs, width, scratch=()):
    cells = counts.shape[0]
    held_args = held(held_args)
    more_args = held(more_args)
    local = pl.BlockSpec(memory_space=pltpu.VMEM)
    return pl.pallas_call(
        kernel,
        in_specs=[local] * len(held_args)
        + [pl.BlockSpec(memory_space=pl.ANY)]
        + [local] * len(more_args),
        out_specs=[local] * len(outs),
        out_shape=[pltpu.VMEM(shape, kind) for shape, kind in outs],
        scratch_shapes=[pltpu.VMEM((cells, width), counts.dtype), pltpu.SemaphoreType.DMA((8,))]
        + [pltpu.VMEM(shape, kind) for shape, kind in scratch],
        cost_estimate=cost(cells, held_args[0].shape[1], width),
        compiler_params=pltpu.CompilerParams(vmem_limit_bytes=LIMIT),
    )(*held_args, counts, *more_args)


def h_partial(start, wt_rel, w_rel, pieces, counts, width):
    half = wt_rel.shape[0] // 2
    outs = [((half, width), F32), ((half, width), BF16)]
    kernel = functools.partial(h_kernel, start=start)
    return call(kernel, [wt_rel, w_rel, *pieces], counts, [], outs, width)


def w_partial(start, w_rel, pieces, counts, width, running, pick):
    cells, rank = w_rel.shape
    last = pick is not None
    sums = [((cells, rank), F32), ((8, rank), F32)]
    outs = [((cells + 16, rank), BF16)] if last else sums
    kernel = functools.partial(
        w_kernel, count=len(pieces), start=start, first=not running, last=last
    )
    more = list(running) + ([pick] if last else [])
    out = call(kernel, [w_rel, *pieces], counts, more, outs, width, sums if last else ())
    return out[0] if last else out


def per_device(counts, w_factor, h_factor, *, devices, gene_devices):
    rows, genes = h_factor.shape
    cells, rank = w_factor.shape
    chips = devices // 2
    across = 2 ** ((chips.bit_length() - 1) // 2)
    along = chips // across
    block = along * rows
    widths = [genes * share // sum(SPLIT) for share in SPLIT]
    starts = [sum(widths[:i]) for i in range(len(widths))]
    chunks = len(widths)

    index = lax.axis_index("cell")
    core = index % 2
    x_at = (index // 2) % across
    z_at = index // (2 * across)

    def send(value, route):
        return lax.ppermute(value, "cell", [(i, route(i)) for i in range(devices)])

    def swap(value):
        return send(value, lambda i: i ^ 1)

    def shift_x(value, s):
        return send(
            value, lambda i: i % 2 + 2 * ((i // 2 + s) % across) + i // (2 * across) * 2 * across
        )

    def shift_z(value, s):
        return send(value, lambda i: (i + 2 * across * s) % devices)

    place = jnp.arange(rank)
    source = (
        (z_at + place // rows % along) % along * (2 * across * rows)
        + (x_at + place // block % across) % across * (2 * rows)
        + (core + place // (block * across)) % 2 * rows
        + place % rows
    )
    pick = source[:, None] == jnp.arange(rank)[None, :]

    lanes = -(-3 // rows)
    w_rel, wt_rel, sums = prepare(w_factor, pick.astype(BF16), (rows, lanes * rank))

    def gather(own):
        column = [own]
        for s in range(1, along):
            column.append(shift_z(own, along - s))
        column = jnp.concatenate(column, 0)
        mine = [column] + [shift_x(column, across - s) for s in range(1, across)]
        return mine + [swap(piece) for piece in mine]

    def reduce(keep, other):
        total = keep + decode_square(swap(other), H_KNEE)
        sent = encode(total[block:], H_KNEE)
        column = total[:block]
        got = [shift_x(sent[(s - 1) * block : s * block], s) for s in range(1, across)]
        for piece in got:
            column = column + decode(piece, H_KNEE)
        sent = encode(column[rows:], H_KNEE)
        mine = column[:rows]
        got = []
        for s in range(1, along):
            got.append(shift_z(sent[(s - 1) * rows : s * rows], s))
        for piece in got:
            mine = mine + decode(piece, H_KNEE)
        return mine

    gathered = []
    for i in range(chunks):
        own = h_factor[:, starts[i] : starts[i] + widths[i]].astype(BF16)
        if i == chunks - 1:
            own = jnp.concatenate([own, sums], 1)
        gathered.append(gather(own))
    w_totals = jnp.concatenate([piece[:, widths[-1] :] for piece in gathered[-1]], 0).astype(F32)
    w_totals = jnp.sum(jnp.sum(w_totals, axis=0).reshape(lanes, rank), axis=0)
    own_totals = lax.dynamic_slice_in_dim(w_totals, index * rows, rows, 0)[:, None]

    updated = []
    again = []
    for i in range(chunks):
        keep, other = h_partial(starts[i], wt_rel, w_rel, gathered[i], counts, widths[i])
        numerator = reduce(keep, other)
        if updated:
            numerator, _ = lax.optimization_barrier((numerator, updated[-1]))
        new = h_factor[:, starts[i] : starts[i] + widths[i]] * numerator / own_totals
        updated.append(new)
        again.append(gather(new.astype(BF16)))
    h_updated = jnp.concatenate(updated, 1)

    pick = pick.astype(F32)
    running = ()
    for i in range(chunks):
        last = i == chunks - 1 and gene_devices == 2
        running = w_partial(
            starts[i], w_rel, again[i], counts, widths[i], running, pick if last else None
        )
    if gene_devices == 2:
        got = lax.ppermute(running, "gene", [(0, 1), (1, 0)])
        totals = sum(
            side[cells + row : cells + row + 1].astype(F32)
            for row in range(3)
            for side in (running, got)
        )
        kept = decode(running[:cells], W_KNEE)
        kept, got = lax.optimization_barrier((kept, got))
        w_updated = w_factor * (kept + decode(got[:cells], W_KNEE)) * (1.0 / totals)
    else:
        numerator, h_totals = lax.psum(running, "gene")
        ratio = jnp.dot(numerator / h_totals[:1], pick, precision=lax.Precision.HIGHEST)
        w_updated = w_factor * ratio
    return (w_updated, h_updated)


def solution(mesh):
    in_specs = (P("cell", "gene"), P("cell", None), P("cell", "gene"))
    out_specs = (P("cell", None), P("cell", "gene"))

    def body(counts, w_factor, h_factor):
        return per_device(
            counts,
            w_factor,
            h_factor,
            devices=mesh.shape["cell"],
            gene_devices=mesh.shape["gene"],
        )

    return jax.shard_map(
        body, mesh=mesh, in_specs=in_specs, out_specs=out_specs, check_vma=False
    )
```

```python
import functools

import jax
import jax.numpy as jnp
from jax import lax
from jax.experimental import pallas as pl
from jax.experimental.pallas import tpu as pltpu
from jax.sharding import PartitionSpec as P


F32 = jnp.float32
BF16 = jnp.bfloat16
SPACE = pltpu.VMEM
H_SHARES = (1, 1, 2, 4)
W_SHARES = (1, 1, 1, 1)
LIMIT = 40 << 20
SPLIT = (4, 4)
H_KNEE = 2.0**20
W_KNEE = 2.0**17


def encode(value, knee):
    part = jnp.minimum(value * (1.0 / knee), 1.0)
    return (value * part * part * part).astype(BF16)


def decode(code, knee):
    code = code.astype(F32)
    root = knee * lax.rsqrt(lax.rsqrt(code * (1.0 / knee)))
    return jnp.where(code < knee, root, code)


def encode_square(value, knee):
    return (value * jnp.minimum(value * (1.0 / knee), 1.0)).astype(BF16)


def decode_square(code, knee):
    code = code.astype(F32)
    square = code * knee
    return jnp.where(code < knee, square * lax.rsqrt(jnp.maximum(square, 1e-30)), code)


def parts_of(value):
    high = value.astype(BF16)
    rest = value - high.astype(F32)
    middle = rest.astype(BF16)
    low = (rest - middle.astype(F32)).astype(BF16)
    return [part.astype(F32) for part in (high, middle, low)]


def prepare_kernel(w_ref, pick_ref, w_rel_ref, wt_rel_ref, sum_ref):
    w_value = w_ref[...]
    w_copy = w_value.astype(BF16)
    pick = pick_ref[...]
    second = (((1,), (1,)), ((), ()))
    w_rel_ref[...] = lax.dot_general(w_copy, pick, second, preferred_element_type=F32).astype(BF16)
    wt_rel_ref[...] = lax.dot_general(pick, w_copy, second, preferred_element_type=F32).astype(BF16)
    rank = w_ref.shape[1]
    rows = sum_ref.shape[0]
    high, middle, low = parts_of(jnp.sum(w_value, axis=0, keepdims=True))
    for block in range(sum_ref.shape[1] // rank):
        row = lax.broadcasted_iota(jnp.int32, (rows, rank), 0) + block * rows
        value = jnp.where(row == 0, high, jnp.where(row == 1, middle, low))
        sum_ref[:, block * rank : (block + 1) * rank] = jnp.where(row < 3, value, 0.0).astype(BF16)


def prepare(w_factor, pick, sum_shape):
    cells, rank = w_factor.shape
    return pl.pallas_call(
        prepare_kernel,
        out_shape=[
            jax.ShapeDtypeStruct((cells, rank), BF16),
            jax.ShapeDtypeStruct((rank, cells), BF16),
            jax.ShapeDtypeStruct(sum_shape, BF16),
        ],
        compiler_params=pltpu.CompilerParams(vmem_limit_bytes=LIMIT),
        name="prepare",
    )(w_factor, pick)


def streamed(counts_ref, buffer_ref, sems, start, shares):
    width = buffer_ref.shape[1]
    sizes = [width * share // sum(shares) for share in shares]
    copies = []
    at = 0
    for i, size in enumerate(sizes):
        copy = pltpu.make_async_copy(
            counts_ref.at[:, pl.ds(start + at, size)],
            buffer_ref.at[:, pl.ds(at, size)],
            sems.at[i],
        )
        copy.start()
        copies.append((copy, slice(at, at + size)))
        at += size
    return copies


def quotient_of(w_ref, h_tile, block):
    modeled = jnp.dot(w_ref[...], h_tile, preferred_element_type=F32)
    return (block.astype(F32) / modeled).astype(BF16)


def h_kernel(wt_ref, w_ref, *refs, start):
    pieces, (counts_ref, keep_ref, send_ref, buffer_ref, sems) = refs[:-5], refs[-5:]
    keep = keep_ref.shape[0]
    for copy, span in streamed(counts_ref, buffer_ref, sems, start, H_SHARES):
        h_tile = jnp.concatenate([piece[:, span] for piece in pieces], axis=0)
        copy.wait()
        quotient = quotient_of(w_ref, h_tile, buffer_ref[:, span])
        term = jnp.dot(wt_ref[...], quotient, preferred_element_type=F32)
        keep_ref[:, span] = term[:keep]
        send_ref[:, span] = encode_square(term[keep:], H_KNEE)


def w_kernel(w_ref, *refs, count, start, first, last):
    pieces, counts_ref = refs[:count], refs[count]
    if last:
        running, pick_ref = refs[count + 1 : -5], refs[-5]
        out_ref, buffer_ref, sems, total_ref = refs[-4:]
    else:
        running = refs[count + 1 : -3]
        total_ref, buffer_ref, sems = refs[-3:]
    copies = streamed(counts_ref, buffer_ref, sems, start, W_SHARES)
    cells = w_ref.shape[0]
    across = (((1,), (1,)), ((), ()))
    if first:
        total_ref[...] = jnp.zeros_like(total_ref)
    else:
        total_ref[...] = running[0][...]
    for copy, span in copies:
        h_tile = jnp.concatenate([piece[:, span] for piece in pieces], axis=0)
        ones = jnp.ones((16, h_tile.shape[1]), BF16)
        copy.wait()
        quotient = quotient_of(w_ref, h_tile, buffer_ref[:, span])
        quotient = jnp.concatenate([quotient, ones], axis=0)
        total_ref[...] += lax.dot_general(quotient, h_tile, across, preferred_element_type=F32)

    if last:
        exact = lax.Precision.HIGHEST
        total = jnp.dot(
            total_ref[...], pick_ref[...], precision=exact, preferred_element_type=F32
        )
        high, middle, low = parts_of(total[cells : cells + 1])
        out_ref[:cells, :] = encode(total[:cells], W_KNEE)
        row = lax.broadcasted_iota(jnp.int32, (16, total.shape[1]), 0)
        tail = jnp.where(row == 0, high, jnp.where(row == 1, middle, low))
        out_ref[cells:, :] = jnp.where(row < 3, tail, 0.0).astype(BF16)


def cost(cells, rank, width):
    return pl.CostEstimate(
        flops=4 * cells * rank * width, transcendentals=0, bytes_accessed=2 * cells * width
    )


def held(pieces):
    return [pltpu.with_memory_space_constraint(piece, SPACE) for piece in pieces]


def call(kernel, held_args, counts, more_args, outs, width, scratch=()):
    cells = counts.shape[0]
    held_args = held(held_args)
    more_args = held(more_args)
    local = pl.BlockSpec(memory_space=pltpu.VMEM)
    return pl.pallas_call(
        kernel,
        in_specs=[local] * len(held_args)
        + [pl.BlockSpec(memory_space=pl.ANY)]
        + [local] * len(more_args),
        out_specs=[local] * len(outs),
        out_shape=[pltpu.VMEM(shape, kind) for shape, kind in outs],
        scratch_shapes=[pltpu.VMEM((cells, width), counts.dtype), pltpu.SemaphoreType.DMA((8,))]
        + [pltpu.VMEM(shape, kind) for shape, kind in scratch],
        cost_estimate=cost(cells, held_args[0].shape[1], width),
        compiler_params=pltpu.CompilerParams(vmem_limit_bytes=LIMIT),
    )(*held_args, counts, *more_args)


def h_partial(start, wt_rel, w_rel, pieces, counts, width):
    half = wt_rel.shape[0] // 2
    outs = [((half, width), F32), ((half, width), BF16)]
    kernel = functools.partial(h_kernel, start=start)
    return call(kernel, [wt_rel, w_rel, *pieces], counts, [], outs, width)


def w_partial(start, w_rel, pieces, counts, width, running, pick):
    cells, rank = w_rel.shape
    last = pick is not None
    total = [((cells + 16, rank), F32)]
    outs = [((cells + 16, rank), BF16)] if last else total
    kernel = functools.partial(
        w_kernel, count=len(pieces), start=start, first=not running, last=last
    )
    more = list(running) + ([pick] if last else [])
    scratch = total if last else ()
    return call(kernel, [w_rel, *pieces], counts, more, outs, width, scratch)


def per_device(counts, w_factor, h_factor, *, devices, gene_devices):
    rows, genes = h_factor.shape
    cells, rank = w_factor.shape
    chips = devices // 2
    across = 2 ** ((chips.bit_length() - 1) // 2)
    along = chips // across
    block = along * rows
    widths = [genes * share // sum(SPLIT) for share in SPLIT]
    starts = [sum(widths[:i]) for i in range(len(widths))]
    chunks = len(widths)

    index = lax.axis_index("cell")
    core = index % 2
    x_at = (index // 2) % across
    z_at = index // (2 * across)

    def send(value, route):
        return lax.ppermute(value, "cell", [(i, route(i)) for i in range(devices)])

    def swap(value):
        return send(value, lambda i: i ^ 1)

    def shift_x(value, s):
        return send(
            value, lambda i: i % 2 + 2 * ((i // 2 + s) % across) + i // (2 * across) * 2 * across
        )

    def shift_z(value, s):
        return send(value, lambda i: (i + 2 * across * s) % devices)

    place = jnp.arange(rank)
    source = (
        (z_at + place // rows % along) % along * (2 * across * rows)
        + (x_at + place // block % across) % across * (2 * rows)
        + (core + place // (block * across)) % 2 * rows
        + place % rows
    )
    pick = source[:, None] == jnp.arange(rank)[None, :]

    lanes = -(-3 // rows)
    w_rel, wt_rel, sums = prepare(w_factor, pick.astype(BF16), (rows, lanes * rank))

    def gather(own):
        column = [own]
        for s in range(1, along):
            column.append(shift_z(own, along - s))
        column = jnp.concatenate(column, 0)
        mine = [column] + [shift_x(column, across - s) for s in range(1, across)]
        swapped = [swap(column)]
        return mine + swapped + [swap(piece) for piece in mine[1:]]

    def reduce(keep, other):
        total = keep + decode_square(swap(other), H_KNEE)
        sent = encode(total[block:], H_KNEE)
        column = total[:block]
        got = [shift_x(sent[(s - 1) * block : s * block], s) for s in range(1, across)]
        for piece in got:
            column = column + decode(piece, H_KNEE)
        sent = encode(column[rows:], H_KNEE)
        mine = column[:rows]
        got = []
        for s in range(1, along):
            got.append(shift_z(sent[(s - 1) * rows : s * rows], s))
        for piece in got:
            mine = mine + decode(piece, H_KNEE)
        return mine

    gathered = []
    for i in range(chunks):
        source = h_factor
        if i == chunks - 1:
            source, sums = lax.optimization_barrier((source, sums))
        own = source[:, starts[i] : starts[i] + widths[i]].astype(BF16)
        if i == chunks - 1:
            own = jnp.concatenate([own, sums], 1)
        gathered.append(gather(own))
    w_totals = jnp.concatenate([piece[:, widths[-1] :] for piece in gathered[-1]], 0).astype(F32)
    w_totals = jnp.sum(jnp.sum(w_totals, axis=0).reshape(lanes, rank), axis=0)
    own_totals = lax.dynamic_slice_in_dim(w_totals, index * rows, rows, 0)[:, None]

    updated = []
    again = []
    for i in range(chunks):
        keep, other = h_partial(starts[i], wt_rel, w_rel, gathered[i], counts, widths[i])
        numerator = reduce(keep, other)
        if updated:
            numerator, _ = lax.optimization_barrier((numerator, updated[-1]))
        new = h_factor[:, starts[i] : starts[i] + widths[i]] * numerator / own_totals
        updated.append(new)
        again.append(gather(new.astype(BF16)))
    h_updated = jnp.concatenate(updated, 1)

    pick = pick.astype(F32)
    running = ()
    for i in range(chunks):
        last = i == chunks - 1 and gene_devices == 2
        running = w_partial(
            starts[i], w_rel, again[i], counts, widths[i], running, pick if last else None
        )
    running = running[0]
    if gene_devices == 2:
        got = lax.ppermute(running, "gene", [(0, 1), (1, 0)])
        totals = sum(
            side[cells + row : cells + row + 1].astype(F32)
            for row in range(3)
            for side in (running, got)
        )
        kept = decode(running[:cells], W_KNEE)
        kept, got = lax.optimization_barrier((kept, got))
        w_updated = w_factor * (kept + decode(got[:cells], W_KNEE)) * (1.0 / totals)
    else:
        total = lax.psum(running, "gene")
        ratio = jnp.dot(
            total[:cells] / total[cells : cells + 1], pick, precision=lax.Precision.HIGHEST
        )
        w_updated = w_factor * ratio
    return (w_updated, h_updated)


def solution(mesh):
    in_specs = (P("cell", "gene"), P("cell", None), P("cell", "gene"))
    out_specs = (P("cell", None), P("cell", "gene"))

    def body(counts, w_factor, h_factor):
        return per_device(
            counts,
            w_factor,
            h_factor,
            devices=mesh.shape["cell"],
            gene_devices=mesh.shape["gene"],
        )

    return jax.shard_map(
        body, mesh=mesh, in_specs=in_specs, out_specs=out_specs, check_vma=False
    )
```

```python
import functools

import jax
import jax.numpy as jnp
from jax import lax
from jax.experimental import pallas as pl
from jax.experimental.pallas import tpu as pltpu
from jax.sharding import PartitionSpec as P


F32 = jnp.float32
BF16 = jnp.bfloat16
SPACE = pltpu.VMEM
H_SHARES = (1, 1, 2, 4)
W_SHARES = (1, 1, 1, 1)
LIMIT = 40 << 20
SPLIT = (4, 4)
H_KNEE = 2.0**20
W_KNEE = 2.0**17


def encode(value, knee):
    part = jnp.minimum(value * (1.0 / knee), 1.0)
    return (value * part * part * part).astype(BF16)


def decode(code, knee):
    code = code.astype(F32)
    root = knee * lax.rsqrt(lax.rsqrt(code * (1.0 / knee)))
    return jnp.where(code < knee, root, code)


def encode_square(value, knee):
    return (value * jnp.minimum(value * (1.0 / knee), 1.0)).astype(BF16)


def decode_square(code, knee):
    code = code.astype(F32)
    square = code * knee
    return jnp.where(code < knee, square * lax.rsqrt(jnp.maximum(square, 1e-30)), code)


def parts_of(value):
    high = value.astype(BF16)
    rest = value - high.astype(F32)
    middle = rest.astype(BF16)
    low = (rest - middle.astype(F32)).astype(BF16)
    return [part.astype(F32) for part in (high, middle, low)]


def prepare_kernel(w_ref, pick_ref, w_rel_ref, wt_rel_ref, sum_ref):
    w_value = w_ref[...]
    w_copy = w_value.astype(BF16)
    pick = pick_ref[...]
    second = (((1,), (1,)), ((), ()))
    w_rel_ref[...] = lax.dot_general(w_copy, pick, second, preferred_element_type=F32).astype(BF16)
    wt_rel_ref[...] = lax.dot_general(pick, w_copy, second, preferred_element_type=F32).astype(BF16)
    rank = w_ref.shape[1]
    rows = sum_ref.shape[0]
    high, middle, low = parts_of(jnp.sum(w_value, axis=0, keepdims=True))
    for block in range(sum_ref.shape[1] // rank):
        row = lax.broadcasted_iota(jnp.int32, (rows, rank), 0) + block * rows
        value = jnp.where(row == 0, high, jnp.where(row == 1, middle, low))
        sum_ref[:, block * rank : (block + 1) * rank] = jnp.where(row < 3, value, 0.0).astype(BF16)


def prepare(w_factor, pick, sum_shape):
    cells, rank = w_factor.shape
    return pl.pallas_call(
        prepare_kernel,
        out_shape=[
            jax.ShapeDtypeStruct((cells, rank), BF16),
            jax.ShapeDtypeStruct((rank, cells), BF16),
            jax.ShapeDtypeStruct(sum_shape, BF16),
        ],
        compiler_params=pltpu.CompilerParams(vmem_limit_bytes=LIMIT),
        name="prepare",
    )(w_factor, pick)


def streamed(counts_ref, buffer_ref, sems, start, shares):
    width = buffer_ref.shape[1]
    sizes = [width * share // sum(shares) for share in shares]
    copies = []
    at = 0
    for i, size in enumerate(sizes):
        copy = pltpu.make_async_copy(
            counts_ref.at[:, pl.ds(start + at, size)],
            buffer_ref.at[:, pl.ds(at, size)],
            sems.at[i],
        )
        copy.start()
        copies.append((copy, slice(at, at + size)))
        at += size
    return copies


def quotient_of(w_ref, h_tile, block):
    modeled = jnp.dot(w_ref[...], h_tile, preferred_element_type=F32)
    return (block.astype(F32) / modeled).astype(BF16)


def h_kernel(wt_ref, w_ref, *refs, start):
    pieces, (counts_ref, keep_ref, send_ref, buffer_ref, sems) = refs[:-5], refs[-5:]
    keep = keep_ref.shape[0]
    for copy, span in streamed(counts_ref, buffer_ref, sems, start, H_SHARES):
        h_tile = jnp.concatenate([piece[:, span] for piece in pieces], axis=0)
        copy.wait()
        quotient = quotient_of(w_ref, h_tile, buffer_ref[:, span])
        term = jnp.dot(wt_ref[...], quotient, preferred_element_type=F32)
        keep_ref[:, span] = term[:keep]
        send_ref[:, span] = encode_square(term[keep:], H_KNEE)


def w_kernel(w_ref, *refs, count, start, first, last):
    pieces, counts_ref = refs[:count], refs[count]
    if last:
        running, pick_ref = refs[count + 1 : -5], refs[-5]
        out_ref, buffer_ref, sems, total_ref = refs[-4:]
    else:
        running = refs[count + 1 : -3]
        total_ref, buffer_ref, sems = refs[-3:]
    copies = streamed(counts_ref, buffer_ref, sems, start, W_SHARES)
    cells = w_ref.shape[0]
    across = (((1,), (1,)), ((), ()))
    if first:
        total_ref[...] = jnp.zeros_like(total_ref)
    else:
        total_ref[...] = running[0][...]
    for copy, span in copies:
        h_tile = jnp.concatenate([piece[:, span] for piece in pieces], axis=0)
        ones = jnp.ones((16, h_tile.shape[1]), BF16)
        copy.wait()
        quotient = quotient_of(w_ref, h_tile, buffer_ref[:, span])
        quotient = jnp.concatenate([quotient, ones], axis=0)
        total_ref[...] += lax.dot_general(quotient, h_tile, across, preferred_element_type=F32)

    if last:
        exact = lax.Precision.HIGHEST
        total = jnp.dot(
            total_ref[...], pick_ref[...], precision=exact, preferred_element_type=F32
        )
        high, middle, low = parts_of(total[cells : cells + 1])
        out_ref[:cells, :] = encode(total[:cells], W_KNEE)
        row = lax.broadcasted_iota(jnp.int32, (16, total.shape[1]), 0)
        tail = jnp.where(row == 0, high, jnp.where(row == 1, middle, low))
        out_ref[cells:, :] = jnp.where(row < 3, tail, 0.0).astype(BF16)


def cost(cells, rank, width):
    return pl.CostEstimate(
        flops=4 * cells * rank * width, transcendentals=0, bytes_accessed=2 * cells * width
    )


def held(pieces):
    return [pltpu.with_memory_space_constraint(piece, SPACE) for piece in pieces]


def call(kernel, held_args, counts, more_args, outs, width, scratch=()):
    cells = counts.shape[0]
    held_args = held(held_args)
    more_args = held(more_args)
    local = pl.BlockSpec(memory_space=pltpu.VMEM)
    return pl.pallas_call(
        kernel,
        in_specs=[local] * len(held_args)
        + [pl.BlockSpec(memory_space=pl.ANY)]
        + [local] * len(more_args),
        out_specs=[local] * len(outs),
        out_shape=[pltpu.VMEM(shape, kind) for shape, kind in outs],
        scratch_shapes=[pltpu.VMEM((cells, width), counts.dtype), pltpu.SemaphoreType.DMA((8,))]
        + [pltpu.VMEM(shape, kind) for shape, kind in scratch],
        cost_estimate=cost(cells, held_args[0].shape[1], width),
        compiler_params=pltpu.CompilerParams(vmem_limit_bytes=LIMIT),
    )(*held_args, counts, *more_args)


def h_partial(start, wt_rel, w_rel, pieces, counts, width):
    half = wt_rel.shape[0] // 2
    outs = [((half, width), F32), ((half, width), BF16)]
    kernel = functools.partial(h_kernel, start=start)
    return call(kernel, [wt_rel, w_rel, *pieces], counts, [], outs, width)


def w_partial(start, w_rel, pieces, counts, width, running, pick):
    cells, rank = w_rel.shape
    last = pick is not None
    total = [((cells + 16, rank), F32)]
    outs = [((cells + 16, rank), BF16)] if last else total
    kernel = functools.partial(
        w_kernel, count=len(pieces), start=start, first=not running, last=last
    )
    more = list(running) + ([pick] if last else [])
    scratch = total if last else ()
    return call(kernel, [w_rel, *pieces], counts, more, outs, width, scratch)


def per_device(counts, w_factor, h_factor, *, devices, gene_devices):
    rows, genes = h_factor.shape
    cells, rank = w_factor.shape
    chips = devices // 2
    across = 2 ** ((chips.bit_length() - 1) // 2)
    along = chips // across
    block = along * rows
    widths = [genes * share // sum(SPLIT) for share in SPLIT]
    starts = [sum(widths[:i]) for i in range(len(widths))]
    chunks = len(widths)

    index = lax.axis_index("cell")
    core = index % 2
    x_at = (index // 2) % across
    z_at = index // (2 * across)

    def send(value, route):
        return lax.ppermute(value, "cell", [(i, route(i)) for i in range(devices)])

    def swap(value):
        return send(value, lambda i: i ^ 1)

    def shift_x(value, s):
        return send(
            value, lambda i: i % 2 + 2 * ((i // 2 + s) % across) + i // (2 * across) * 2 * across
        )

    def shift_z(value, s):
        return send(value, lambda i: (i + 2 * across * s) % devices)

    place = jnp.arange(rank)
    source = (
        (z_at + place // rows % along) % along * (2 * across * rows)
        + (x_at + place // block % across) % across * (2 * rows)
        + (core + place // (block * across)) % 2 * rows
        + place % rows
    )
    pick = source[:, None] == jnp.arange(rank)[None, :]

    lanes = -(-3 // rows)
    w_rel, wt_rel, sums = prepare(w_factor, pick.astype(BF16), (rows, lanes * rank))

    def gather(own):
        column = [own]
        for s in range(1, along):
            column.append(shift_z(own, along - s))
        column = jnp.concatenate(column, 0)
        mine = [column] + [shift_x(column, across - s) for s in range(1, across)]
        swapped = [swap(column)]
        return mine + swapped + [swap(piece) for piece in mine[1:]]

    def reduce(keep, other):
        total = keep + decode_square(swap(other), H_KNEE)
        sent = encode(total[block:], H_KNEE)
        column = total[:block]
        got = [shift_x(sent[(s - 1) * block : s * block], s) for s in range(1, across)]
        for piece in got:
            column = column + decode(piece, H_KNEE)
        sent = encode(column[rows:], H_KNEE)
        mine = column[:rows]
        got = []
        for s in range(1, along):
            got.append(shift_z(sent[(s - 1) * rows : s * rows], s))
        for piece in got:
            mine = mine + decode(piece, H_KNEE)
        return mine

    gathered = []
    for i in range(chunks):
        own = h_factor[:, starts[i] : starts[i] + widths[i]].astype(BF16)
        if i == chunks - 1:
            own = jnp.concatenate([own, sums], 1)
        gathered.append(gather(own))
    w_totals = jnp.concatenate([piece[:, widths[-1] :] for piece in gathered[-1]], 0).astype(F32)
    w_totals = jnp.sum(jnp.sum(w_totals, axis=0).reshape(lanes, rank), axis=0)
    own_totals = lax.dynamic_slice_in_dim(w_totals, index * rows, rows, 0)[:, None]

    updated = []
    again = []
    for i in range(chunks):
        keep, other = h_partial(starts[i], wt_rel, w_rel, gathered[i], counts, widths[i])
        numerator = reduce(keep, other)
        if updated:
            numerator, _ = lax.optimization_barrier((numerator, updated[-1]))
        new = h_factor[:, starts[i] : starts[i] + widths[i]] * numerator / own_totals
        updated.append(new)
        again.append(gather(new.astype(BF16)))
    h_updated = jnp.concatenate(updated, 1)

    pick = pick.astype(F32)
    running = ()
    for i in range(chunks):
        last = i == chunks - 1 and gene_devices == 2
        running = w_partial(
            starts[i], w_rel, again[i], counts, widths[i], running, pick if last else None
        )
    running = running[0]
    if gene_devices == 2:
        got = lax.ppermute(running, "gene", [(0, 1), (1, 0)])
        totals = sum(
            side[cells + row : cells + row + 1].astype(F32)
            for row in range(3)
            for side in (running, got)
        )
        kept = decode(running[:cells], W_KNEE)
        kept, got = lax.optimization_barrier((kept, got))
        w_updated = w_factor * (kept + decode(got[:cells], W_KNEE)) * (1.0 / totals)
    else:
        total = lax.psum(running, "gene")
        ratio = jnp.dot(
            total[:cells] / total[cells : cells + 1], pick, precision=lax.Precision.HIGHEST
        )
        w_updated = w_factor * ratio
    return (w_updated, h_updated)


def solution(mesh):
    in_specs = (P("cell", "gene"), P("cell", None), P("cell", "gene"))
    out_specs = (P("cell", None), P("cell", "gene"))

    def body(counts, w_factor, h_factor):
        return per_device(
            counts,
            w_factor,
            h_factor,
            devices=mesh.shape["cell"],
            gene_devices=mesh.shape["gene"],
        )

    return jax.shard_map(
        body, mesh=mesh, in_specs=in_specs, out_specs=out_specs, check_vma=False
    )
```
